32 devices in a mesh: tok: 2 (over x), blk: 16 (over z, y, core).
Axes of the slice: x: 2, y: 2, z: 4, core: 2. Of those that a mesh axis runs over, the one named last changes fastest.
Arguments:
- hidden_in: bfloat16 [16, 256, 1024], P('blk', 'tok'), may hold values from -22 to 22
- seg_ids: int32 [16, 256], P('blk'), may hold values from 0 to 3, never falling along the last dimension, each value on 1 to 128 neighbouring positions
- norm_gain1: float32 [1024], replicated, may hold values from 0.1 to 1.9
- w_query: bfloat16 [1024, 1024], replicated, may hold values from -0.0234375 to 0.0234375
- w_key_value: bfloat16 [1024, 2048], replicated, may hold values from -0.1875 to 0.1875
- rel_bias: float32 [32, 16], replicated, may hold values from -3 to 300
- w_attn_out: bfloat16 [1024, 1024], replicated, may hold values from -0.1875 to 0.1875
- norm_gain2: float32 [1024], replicated, may hold values from 0.1 to 1.9
- w_in: bfloat16 [4096, 1024], P('blk'), may hold values from -0.1875 to 0.1875
- w_out: bfloat16 [4096, 1024], P('blk'), may hold values from -0.09375 to 0.09375
Outputs:
- layer_out: bfloat16 [16, 256, 1024], P('blk', 'tok')
The draws below stay inside these ranges and needn't reach their ends.
Inputs may be any that keep to these rules, and one draw needn't show every extreme that they name: `seg_ids`: in each stream the segment numbers never fall; each of the 4 segments is a run of 1 to 128 tokens, one exactly 128 long.
All inputs are finite; a program needn't handle non-finite values.
Results may differ from the reference program's by a relative error of at most 0.007.
Values may be sent and summed in bfloat16 or wider, within the bound.
A program may use at most 192 MiB of HBM per device.

```python
import math
import jax
import jax.numpy as jnp
import numpy as np
from jax import lax

D = 1024
HEADS = 16
HD = 64
FF = 4096
BUCKETS = 32
SEGS = 4
SEQ = 256
STREAMS = 16
MOST_SEG = 128
N_BLK = 16


def draw_hidden_in(key, part):
    base_key = jax.random.fold_in(key, 11)
    row_key = jax.random.fold_in(key, 12)
    column_key = jax.random.fold_in(key, 13)
    shape = (STREAMS, SEQ, D)
    column_scale = jnp.exp(jax.random.uniform(column_key, (D,), jnp.float32, -1.15, 1.15))
    base = jax.random.truncated_normal(base_key, -3.0, 3.0, shape, jnp.float32)
    row_scale = jnp.exp(jax.random.uniform(row_key, (STREAMS, SEQ, 1), jnp.float32, -0.69, 0.69))
    return (base * row_scale * column_scale).astype(jnp.bfloat16)


def draw_rel_bias(key, part):
    base = jax.random.uniform(jax.random.fold_in(key, 21), (BUCKETS, HEADS), jnp.float32, -3.0, 3.0)
    return base


def steps_of(stream_key, extent, split, least, top_value):
    loudness, own = 1.0, jax.random.fold_in(stream_key, 6)
    for position, shards_of in split:
        heights = jnp.exp(jax.random.uniform(jax.random.fold_in(own, position), (shards_of,), jnp.float32, least / len(split), top_value / len(split)))
        loudness = loudness * jnp.repeat(heights, extent[position] // shards_of).reshape([-1 if axis == position else 1 for axis in range(len(extent))])
    return loudness


def split_up(number_of, total, bound, skew):
    weights = [(1 << 20) // math.isqrt(standing ** skew) + 1 for standing in range(2, number_of + 1)]
    spare, counts = total - bound - (number_of - 1), [1] * (number_of - 1)
    while spare > 0:
        candidates = [i for i in range(number_of - 1) if counts[i] < bound]
        pool, budget = sum([weights[i] for i in candidates]), spare
        for i in candidates:
            addition = min(bound - counts[i], max(1, budget * weights[i] // pool), spare)
            counts[i] = counts[i] + addition
            spare = spare - addition
    return np.array([bound] + counts)


def uneven_parts(rng, amount, total, most, slope):
    if amount == 2:
        one = jax.random.randint(rng, (), max(1, total - most), min(most, total - 1) + 1)
        return jnp.stack([one, total - one])
    sizes = jnp.asarray(split_up(amount, total, most, slope), jnp.int32)
    couples = (amount - 1) // 2
    giver, sink = sizes[1:1 + 2 * couples:2], sizes[2:2 + 2 * couples:2]
    room = jnp.minimum(giver - 1, most - sink)
    passed = jax.random.randint(jax.random.fold_in(rng, 1), (couples,), 0, 1 << 20) % (room + 1)
    sizes = sizes.at[1:1 + 2 * couples:2].set(giver - passed).at[2:2 + 2 * couples:2].set(sink + passed)
    return sizes[jax.random.permutation(jax.random.fold_in(rng, 2), amount)]


def gaussian(stream_key, shape, deviation, most, shards=(), held_as=jnp.bfloat16):
    level = steps_of(stream_key, shape, shards, -0.22, 0.18) if shards else 1.0
    entries = jax.random.normal(stream_key, shape, jnp.float32) * deviation * level
    return jnp.minimum(jnp.maximum(entries, -most), most).astype(held_as)


def setup_inputs(seed: int = 0) -> dict:
    keys = jax.random.split(jax.random.key(seed), 11)
    return {
        "hidden_in": draw_hidden_in(jax.random.fold_in(keys[10], 71), 0),
        "seg_ids": jax.vmap(lambda own: jnp.searchsorted(jnp.cumsum(uneven_parts(own, SEGS, SEQ, MOST_SEG, 2)), jnp.arange(SEQ), side="right"))(jax.random.split(keys[1], STREAMS)).reshape((STREAMS, SEQ)).astype(jnp.int32),
        "norm_gain1": jnp.clip(1.0 + 0.18 * jax.random.normal(keys[2], (D,), jnp.float32), 0.1, 1.9),
        "w_query": gaussian(keys[3], (D, D), (D * HD) ** -0.5, 0.0234375),
        "w_key_value": gaussian(keys[4], (D, 2 * D), D ** -0.5, 0.1875),
        "rel_bias": draw_rel_bias(jax.random.fold_in(keys[10], 71), 0),
        "w_attn_out": gaussian(keys[6], (D, D), D ** -0.5, 0.1875),
        "norm_gain2": jnp.clip(1.0 + 0.18 * jax.random.normal(keys[7], (D,), jnp.float32), 0.1, 1.9),
        "w_in": gaussian(keys[8], (FF, D), D ** -0.5, 0.1875, ((0, 16),)),
        "w_out": gaussian(keys[9], (FF, D), FF ** -0.5, 0.09375, ((0, 16),)),
    }


bucket_bounds = (12, 16, 23, 32, 46, 64, 91)
epsilon = 1e-06

def bucket_of(offset):
    distance = jnp.abs(offset)
    far_bucket = jnp.full_like(distance, 8)
    for boundary in bucket_bounds:
        far_bucket = far_bucket + (distance >= boundary).astype(jnp.int32)
    chosen = jnp.where(distance < 8, distance, far_bucket)
    return chosen + 16 * (offset > 0).astype(jnp.int32)

def rms_scale(values, gain):
    mean_square = lax.optimization_barrier(jnp.mean(values * values, axis=-1, keepdims=True))
    return values * lax.rsqrt(mean_square + epsilon) * gain

def reference(hidden_in, seg_ids, norm_gain1, w_query, w_key_value, rel_bias, w_attn_out, norm_gain2, w_in, w_out):
    positions = jnp.arange(SEQ, dtype=jnp.int32)
    bucket_grid = bucket_of(positions[None, :] - positions[:, None])
    bias_grid = jnp.take(jnp.transpose(rel_bias), bucket_grid, axis=1)
    slice_width = FF // N_BLK

    def one_stream(operands):
        stream_in, segment_row = operands
        hidden = stream_in.astype(jnp.float32)
        normed = rms_scale(hidden, norm_gain1).astype(jnp.bfloat16)
        queries = jnp.dot(normed, w_query, preferred_element_type=jnp.float32).astype(jnp.bfloat16).reshape(SEQ, HEADS, HD)
        keys_values = jnp.dot(normed, w_key_value, preferred_element_type=jnp.float32).astype(jnp.bfloat16)
        key_heads = keys_values[:, :D].reshape(SEQ, HEADS, HD)
        value_heads = keys_values[:, D:].reshape(SEQ, HEADS, HD)
        scores = jnp.einsum('qhd,khd->hqk', queries.astype(jnp.float32), key_heads.astype(jnp.float32)) + bias_grid
        same_segment = (segment_row[:, None] == segment_row[None, :])[None]
        masked = jnp.where(same_segment, scores, -1e+30)
        row_max = lax.optimization_barrier(jnp.max(masked, axis=-1, keepdims=True))
        exps = jnp.where(same_segment, jnp.exp(masked - row_max), 0.0)
        denominator = lax.optimization_barrier(jnp.sum(exps, axis=-1))
        weights = exps.astype(jnp.bfloat16)
        mixed = jnp.einsum('hqk,khd->hqd', weights.astype(jnp.float32), value_heads.astype(jnp.float32)) / denominator[..., None]
        attended = jnp.transpose(mixed, (1, 0, 2)).reshape(SEQ, D).astype(jnp.bfloat16)
        middle = hidden + jnp.dot(attended, w_attn_out, preferred_element_type=jnp.float32)
        normed_two = rms_scale(middle, norm_gain2).astype(jnp.bfloat16)
        inner = jax.nn.relu(lax.dot_general(normed_two, w_in, (((1,), (1,)), ((), ())), preferred_element_type=jnp.float32)).astype(jnp.bfloat16)
        inner_groups = inner.reshape(SEQ, N_BLK, slice_width).astype(jnp.float32)
        out_groups = w_out.reshape(N_BLK, slice_width, D).astype(jnp.float32)
        partials = jnp.einsum('sjf,jfd->jsd', inner_groups, out_groups).astype(jnp.bfloat16)
        partials = lax.optimization_barrier(partials)
        feed = lax.optimization_barrier(jnp.sum(partials.astype(jnp.float32), axis=0))
        return (middle + feed).astype(jnp.bfloat16)
    return lax.map(one_stream, (hidden_in, seg_ids))
```

```python
import functools

import jax
import jax.numpy as jnp
from jax import lax
from jax.experimental import pallas as pl
from jax.experimental.pallas import tpu as pltpu
from jax.sharding import PartitionSpec as P

D = 1024
HEADS = 16
HD = 64
BUCKETS = 32

bucket_bounds = (12, 16, 23, 32, 46, 64, 91)
epsilon = 1e-06
MESH = pl.DeviceIdType.MESH
VM = pl.BlockSpec(memory_space=pltpu.VMEM)


def bucket_of(offset):
    distance = jnp.abs(offset)
    far_bucket = jnp.full_like(distance, 8)
    for boundary in bucket_bounds:
        far_bucket = far_bucket + (distance >= boundary).astype(jnp.int32)
    chosen = jnp.where(distance < 8, distance, far_bucket)
    return chosen + 16 * (offset > 0).astype(jnp.int32)


def rms_scale(values, gain):
    mean_square = jnp.mean(values * values, axis=-1, keepdims=True)
    return values * lax.rsqrt(mean_square + epsilon) * gain


def exchange_kernel(n_tok, x_ref, o_ref, send_sem, recv_sem, own_sem):
    me = lax.axis_index("tok")
    barrier = pltpu.get_barrier_semaphore()
    for d in range(1, n_tok):
        pl.semaphore_signal(
            barrier, inc=1, device_id={"tok": lax.rem(me + d, n_tok)}, device_id_type=MESH
        )
    own = pltpu.make_async_copy(x_ref, o_ref.at[me], own_sem)
    own.start()
    pl.semaphore_wait(barrier, n_tok - 1)
    copies = []
    for d in range(1, n_tok):
        copy = pltpu.make_async_remote_copy(
            src_ref=x_ref,
            dst_ref=o_ref.at[me],
            send_sem=send_sem.at[d],
            recv_sem=recv_sem.at[d],
            device_id={"tok": lax.rem(me + d, n_tok)},
            device_id_type=MESH,
        )
        copy.start()
        copies.append(copy)
    own.wait()
    for copy in copies:
        copy.wait()


def exchange(x, n_tok):
    rows = x.shape[0]
    return pl.pallas_call(
        functools.partial(exchange_kernel, n_tok),
        out_shape=jax.ShapeDtypeStruct((n_tok, rows, D), jnp.bfloat16),
        in_specs=[VM],
        out_specs=VM,
        scratch_shapes=[
            pltpu.SemaphoreType.DMA((n_tok,)),
            pltpu.SemaphoreType.DMA((n_tok,)),
            pltpu.SemaphoreType.DMA,
        ],
        compiler_params=pltpu.CompilerParams(collective_id=0, has_side_effects=True),
    )(x)


def attention_kernel(
    hid_ref, seg_row_ref, seg_col_ref, g1_ref, wq_ref, wkv_ref, bias_ref, wo_ref, g2_ref,
    mid_ref, n2_ref, q_scr, kv_scr, att_scr,
):
    tok = lax.axis_index("tok")
    n_tok, rows, _ = hid_ref.shape
    count = n_tok * rows
    wide = 2 * count
    for part in range(n_tok):
        normed = rms_scale(hid_ref[part].astype(jnp.float32), g1_ref[...]).astype(jnp.bfloat16)
        kv_scr[part * rows:(part + 1) * rows, :] = jnp.dot(
            normed, wkv_ref[...], preferred_element_type=jnp.float32
        ).astype(jnp.bfloat16)
    hidden = hid_ref[tok].astype(jnp.float32)
    normed = rms_scale(hidden, g1_ref[...]).astype(jnp.bfloat16)
    q_scr[...] = jnp.dot(normed, wq_ref[...], preferred_element_type=jnp.float32).astype(
        jnp.bfloat16
    )
    spot = lax.broadcasted_iota(jnp.int32, (BUCKETS, wide), 1)
    offset = jnp.where(spot < count, spot, spot - wide) - tok * rows
    chosen = lax.broadcasted_iota(jnp.int32, (BUCKETS, wide), 0) == bucket_of(offset)
    bias_line = jnp.dot(
        bias_ref[...], chosen.astype(jnp.float32),
        precision=lax.Precision.HIGHEST, preferred_element_type=jnp.float32,
    )
    same = seg_col_ref[...] == seg_row_ref[...]
    lane = lax.broadcasted_iota(jnp.int32, (rows, 2 * HD), 1)
    low = lane < HD
    for pair in range(HEADS // 2):
        at = pair * 2 * HD
        q_two = q_scr[:, at:at + 2 * HD]
        k_two = kv_scr[:, at:at + 2 * HD]
        v_two = kv_scr[:, D + at:D + at + 2 * HD]
        halves = []
        for half in range(2):
            head = 2 * pair + half
            keep = low if half == 0 else jnp.logical_not(low)
            q_one = jnp.where(keep, q_two, jnp.zeros_like(q_two))
            scores = lax.dot_general(
                q_one, k_two, (((1,), (1,)), ((), ())), preferred_element_type=jnp.float32
            )
            line = jnp.broadcast_to(bias_line[head:head + 1, :], (rows, wide))
            bias = pltpu.roll(line, 0, 1, stride=1, stride_axis=0)[:, :count]
            masked = jnp.where(same, scores + bias, -1e30)
            top = jnp.max(masked, axis=-1, keepdims=True)
            exps = jnp.exp(masked - top)
            total = jnp.sum(exps, axis=-1, keepdims=True)
            mixed = jnp.dot(exps.astype(jnp.bfloat16), v_two, preferred_element_type=jnp.float32)
            halves.append(mixed / total)
        att_scr[:, at:at + 2 * HD] = jnp.where(low, halves[0], halves[1]).astype(jnp.bfloat16)
    middle = hidden + jnp.dot(att_scr[...], wo_ref[...], preferred_element_type=jnp.float32)
    mid_ref[...] = middle
    n2_ref[...] = rms_scale(middle, g2_ref[...]).astype(jnp.bfloat16)


def attention(hid, seg_row, seg_col, g1, wq, wkv, bias_t, wo, g2):
    n_tok, rows, _ = hid.shape
    return pl.pallas_call(
        attention_kernel,
        out_shape=(
            jax.ShapeDtypeStruct((rows, D), jnp.float32),
            jax.ShapeDtypeStruct((rows, D), jnp.bfloat16),
        ),
        in_specs=[VM] * 9,
        out_specs=(VM, VM),
        scratch_shapes=[
            pltpu.VMEM((rows, D), jnp.bfloat16),
            pltpu.VMEM((n_tok * rows, 2 * D), jnp.bfloat16),
            pltpu.VMEM((rows, D), jnp.bfloat16),
        ],
        compiler_params=pltpu.CompilerParams(vmem_limit_bytes=48 << 20),
    )(hid, seg_row, seg_col, g1, wq, wkv, bias_t, wo, g2)


def mlp_kernel(
    DEEP, WIDE, n2_ref, win_ref, wout_ref, mid_ref, out_ref,
    gath, part, cross, side_in, chain_in, acc,
    s_chain, s_side, s_core, r_gath, s_cross, r_cross, s_ret, r_ret, s_sum, r_sum,
):
    blk = lax.axis_index("blk")
    c = lax.rem(blk, 2)
    chip = blk // 2
    y = lax.rem(chip, WIDE)
    z = chip // WIDE
    rows = n2_ref.shape[0]
    oc = 1 - c

    def dev(zz, yy, cc):
        return {"blk": (zz * WIDE + yy) * 2 + cc}

    def remote(src, dst, ss, rs, to):
        return pltpu.make_async_remote_copy(
            src_ref=src, dst_ref=dst, send_sem=ss, recv_sem=rs, device_id=to, device_id_type=MESH
        )

    has_up = z < DEEP - 1
    has_down = z > 0

    barrier = pltpu.get_barrier_semaphore()
    pl.semaphore_signal(barrier, inc=1, device_id=dev(z, y, oc), device_id_type=MESH)
    for d in range(1, WIDE):
        pl.semaphore_signal(
            barrier, inc=1, device_id=dev(z, lax.rem(y + d, WIDE), c), device_id_type=MESH
        )

    @pl.when(has_up)
    def _():
        pl.semaphore_signal(barrier, inc=1, device_id=dev(z + 1, y, c), device_id_type=MESH)

    @pl.when(has_down)
    def _():
        pl.semaphore_signal(barrier, inc=1, device_id=dev(z - 1, y, c), device_id_type=MESH)

    gath[chip, c] = n2_ref[...]
    ends = jnp.where(has_up, 1, 0) + jnp.where(has_down, 1, 0)
    pl.semaphore_wait(barrier, WIDE + ends)

    def pass_on(i, core, to, ss):
        return remote(gath.at[i, core], gath.at[i, core], ss, r_gath.at[i, core], to)

    def arrived(i, core):
        pass_on(i, core, dev(z, y, oc), s_core.at[i]).wait_recv()

    def up(i):
        return pass_on(i, c, dev(z + 1, y, c), s_chain.at[0, i // WIDE])

    def down(i):
        return pass_on(i, c, dev(z - 1, y, c), s_chain.at[1, i // WIDE])

    def side(i, d):
        return pass_on(i, c, dev(z, lax.rem(y + d, WIDE), c), s_side.at[d, i // WIDE])

    def core(i):
        return pass_on(i, c, dev(z, y, oc), s_core.at[i])

    sense = 1 - 2 * lax.rem(z, 2)
    if DEEP == 4:
        inner_place = lax.rem((z + 1) // 2, 2)
        reach = [sense * (j * (1 - inner_place) + (0, 1, -1, -2)[j] * inner_place) for j in range(4)]
        order = [z + r for r in reach]
    else:
        order = [lax.rem(z + j, DEEP) for j in range(DEEP)]

    def stage_column(j):
        zz = order[j]
        i = zz * WIDE + y
        if j > 0:
            arrived(i, c)

            @pl.when(jnp.logical_and(zz < z, has_up))
            def _():
                up(i).start()

            @pl.when(jnp.logical_and(zz > z, has_down))
            def _():
                down(i).start()
        else:

            @pl.when(has_up)
            def _():
                up(i).start()

            @pl.when(has_down)
            def _():
                down(i).start()
        for d in range(1, WIDE):
            side(i, d).start()
        core(i).start()

    def stage_side(j):
        for d in range(1, WIDE):
            i = order[j] * WIDE + lax.rem(y + d, WIDE)
            arrived(i, c)
            core(i).start()

    def cross_copy(i):
        return remote(part.at[i, oc], cross.at[i], s_cross.at[i], r_cross.at[i], dev(z, y, oc))

    def stage_compute(j):
        def one(d, carry):
            i = order[j] * WIDE + lax.rem(y + d, WIDE)
            arrived(i, oc)
            tokens = gath[i].reshape(2 * rows, D)
            hidden = lax.dot_general(
                tokens, win_ref[...], (((1,), (1,)), ((), ())), preferred_element_type=jnp.float32
            )
            hidden = jnp.maximum(hidden, 0.0).astype(jnp.bfloat16)
            terms = jnp.dot(hidden, wout_ref[...], preferred_element_type=jnp.float32)
            part[i] = terms.astype(jnp.bfloat16).reshape(2, rows, D)
            cross_copy(i).start()
            return carry

        lax.fori_loop(1, WIDE + 1, one, 0)

    def both_cores(i):
        cross_copy(i).wait_recv()
        return part[i, c].astype(jnp.float32) + cross[i].astype(jnp.float32)

    def ret_copy(j, d):
        i = order[j] * WIDE + lax.rem(y + d, WIDE)
        return remote(
            part.at[i, c], side_in.at[d - 1, order[j]],
            s_ret.at[d - 1, order[j]], r_ret.at[d - 1, order[j]],
            dev(z, lax.rem(y + d, WIDE), c),
        )

    def stage_return(j):
        for d in range(1, WIDE):
            i = order[j] * WIDE + lax.rem(y + d, WIDE)
            part[i, c] = both_cores(i).astype(jnp.bfloat16)
            ret_copy(j, d).start()

    def column_sum(j):
        total = both_cores(order[j] * WIDE + y)
        for d in range(1, WIDE):
            ret_copy(j, d).wait_recv()
            total = total + side_in[d - 1, order[j]].astype(jnp.float32)
        return total

    def sum_up(target):
        return remote(
            part.at[target * WIDE + y, c], chain_in.at[target],
            s_sum.at[target], r_sum.at[target], dev(z + 1, y, c),
        )

    def sum_down(target):
        slot = jnp.where(target == z - 1, DEEP, target)
        return remote(
            part.at[target * WIDE + y, c], chain_in.at[slot],
            s_sum.at[target], r_sum.at[slot], dev(z - 1, y, c),
        )

    def sum_arrived(slot):
        remote(
            chain_in.at[slot], chain_in.at[slot], s_sum.at[0], r_sum.at[slot], dev(z, y, oc)
        ).wait_recv()
        return chain_in[slot].astype(jnp.float32)

    stage_column(0)
    for j in range(DEEP):
        if j + 1 < DEEP:
            stage_column(j + 1)
        stage_side(j)
        stage_compute(j)
        if j > 0:
            stage_return(j - 1)
    stage_return(DEEP - 1)

    for j in range(DEEP - 1, 0, -1):
        target = order[j]
        i = target * WIDE + y
        acc[...] = column_sum(j)
        upward = target > z

        @pl.when(jnp.where(upward, has_down, has_up))
        def _():
            acc[...] += sum_arrived(target)

        part[i, c] = acc[...].astype(jnp.bfloat16)

        @pl.when(upward)
        def _():
            sum_up(target).start()

        @pl.when(jnp.logical_not(upward))
        def _():
            sum_down(target).start()

    acc[...] = mid_ref[...] + column_sum(0)

    @pl.when(has_down)
    def _():
        acc[...] += sum_arrived(z)

    @pl.when(has_up)
    def _():
        acc[...] += sum_arrived(DEEP)

    out_ref[...] = acc[...].astype(jnp.bfloat16)

    for j in range(DEEP):
        i = order[j] * WIDE + y
        goes_up = has_up if j == 0 else jnp.logical_and(order[j] < z, has_up)
        goes_down = has_down if j == 0 else jnp.logical_and(order[j] > z, has_down)

        @pl.when(goes_up)
        def _():
            up(i).wait_send()

        @pl.when(goes_down)
        def _():
            down(i).wait_send()

        for d in range(1, WIDE):
            side(i, d).wait_send()
            ret_copy(j, d).wait_send()
        for d in range(WIDE):
            k = order[j] * WIDE + lax.rem(y + d, WIDE)
            core(k).wait_send()
            cross_copy(k).wait_send()
        if j > 0:

            @pl.when(order[j] > z)
            def _():
                sum_up(order[j]).wait_send()

            @pl.when(order[j] < z)
            def _():
                sum_down(order[j]).wait_send()


def mlp(n2, w_in, w_out, middle, n_blk):
    rows = n2.shape[0]
    deep = 4
    wide = n_blk // (2 * deep)
    chips = deep * wide
    spread = max(wide - 1, 1)
    dma = pltpu.SemaphoreType.DMA
    return pl.pallas_call(
        functools.partial(mlp_kernel, deep, wide),
        out_shape=jax.ShapeDtypeStruct((rows, D), jnp.bfloat16),
        in_specs=[VM] * 4,
        out_specs=VM,
        scratch_shapes=[
            pltpu.VMEM((chips, 2, rows, D), jnp.bfloat16),
            pltpu.VMEM((chips, 2, rows, D), jnp.bfloat16),
            pltpu.VMEM((chips, rows, D), jnp.bfloat16),
            pltpu.VMEM((spread, deep, rows, D), jnp.bfloat16),
            pltpu.VMEM((deep + 1, rows, D), jnp.bfloat16),
            pltpu.VMEM((rows, D), jnp.float32),
            dma((2, deep)),
            dma((wide, deep)),
            dma((chips,)),
            dma((chips, 2)),
            dma((chips,)),
            dma((chips,)),
            dma((spread, deep)),
            dma((spread, deep)),
            dma((deep + 1,)),
            dma((deep + 1,)),
        ],
        compiler_params=pltpu.CompilerParams(
            collective_id=1, has_side_effects=True, vmem_limit_bytes=60 << 20
        ),
    )(n2, w_in, w_out, middle)


def per_device(
    n_tok, n_blk, hidden_in, seg_ids, norm_gain1, w_query, w_key_value, rel_bias, w_attn_out,
    norm_gain2, w_in, w_out,
):
    hid = exchange(hidden_in[0], n_tok)
    rows = hidden_in.shape[1]
    seg_row = seg_ids
    start = lax.axis_index("tok") * rows
    seg_col = lax.dynamic_slice_in_dim(seg_ids[0], start, rows)[:, None]
    middle, n2 = attention(
        hid, seg_row, seg_col, norm_gain1[None], w_query, w_key_value, jnp.transpose(rel_bias),
        w_attn_out, norm_gain2[None],
    )
    return mlp(n2, w_in, w_out, middle, n_blk)[None]


def solution(mesh):
    placed = (
        P("blk", "tok", None),
        P("blk", None),
        P(),
        P(),
        P(),
        P(),
        P(),
        P(),
        P("blk", None),
        P("blk", None),
    )
    return jax.shard_map(
        functools.partial(per_device, mesh.shape["tok"], mesh.shape["blk"]),
        mesh=mesh, in_specs=placed, out_specs=P("blk", "tok", None), check_vma=False,
    )
```

```python
import functools

import jax
import jax.numpy as jnp
from jax import lax
from jax.experimental import pallas as pl
from jax.experimental.pallas import tpu as pltpu
from jax.sharding import PartitionSpec as P

D = 1024
HEADS = 16
HD = 64
BUCKETS = 32

bucket_bounds = (12, 16, 23, 32, 46, 64, 91)
epsilon = 1e-06
MESH = pl.DeviceIdType.MESH
VM = pl.BlockSpec(memory_space=pltpu.VMEM)
ANY = pl.BlockSpec(memory_space=pl.ANY)


def bucket_of(offset):
    distance = jnp.abs(offset)
    far_bucket = jnp.full_like(distance, 8)
    for boundary in bucket_bounds:
        far_bucket = far_bucket + (distance >= boundary).astype(jnp.int32)
    chosen = jnp.where(distance < 8, distance, far_bucket)
    return chosen + 16 * (offset > 0).astype(jnp.int32)


def rms_scale(values, gain):
    mean_square = jnp.mean(values * values, axis=-1, keepdims=True)
    return values * lax.rsqrt(mean_square + epsilon) * gain


def layer_kernel(
    WIDE,
    x_ref, seg_row_ref, seg_col_ref, g1_ref, bias_ref, g2_ref, wq_hbm, wkv_hbm, wo_hbm, win_hbm,
    wout_hbm, out_ref,
    wq, wkv, wo, win, wout, hid, q_scr, kv_scr, att_scr, mid, gath, part, cross, inbox,
    s_load, s_hid, r_hid, s_far, s_near, r_w, s_z, s_y, s_core, r_gath, s_cross, r_cross,
    s_out, r_in,
):
    tok = lax.axis_index("tok")
    blk = lax.axis_index("blk")
    c = lax.rem(blk, 2)
    chip = blk // 2
    y = lax.rem(chip, WIDE)
    z = chip // WIDE
    zp = z + 1 - 2 * lax.rem(z, 2)
    zq = lax.rem(z + 2, 4)
    oc = 1 - c
    n_tok, rows, _ = hid.shape
    count = n_tok * rows
    wide = 2 * count
    half_rows = rows // 2
    piece = win_hbm.shape[0] // n_tok

    def dev(zz, yy, cc):
        return {"blk": (zz * WIDE + yy) * 2 + cc}

    def place(zz, yy):
        return lax.rem(zz, 2) * WIDE + yy

    def beside(d):
        return lax.rem(y + d, WIDE)

    def other_tok(d):
        return lax.rem(tok + d, n_tok)

    def remote(src, dst, ss, rs, to):
        return pltpu.make_async_remote_copy(
            src_ref=src, dst_ref=dst, send_sem=ss, recv_sem=rs, device_id=to, device_id_type=MESH
        )

    sides = range(1, WIDE)
    toks = range(1, n_tok)
    core_dev = dev(z, y, oc)
    near_dev = dev(zp, y, c)
    far_dev = dev(zq, y, c)

    barrier = pltpu.get_barrier_semaphore()
    greet = [core_dev, near_dev, far_dev]
    greet += [dev(z, beside(d), c) for d in sides] + [{"tok": other_tok(d)} for d in toks]
    for to in greet:
        pl.semaphore_signal(barrier, inc=1, device_id=to, device_id_type=MESH)

    loads = [
        pltpu.make_async_copy(src, dst, s_load.at[k])
        for k, (src, dst) in enumerate(
            [(wq_hbm, wq), (wkv_hbm, wkv), (wo_hbm, wo), (win_hbm, win.at[0]), (wout_hbm, wout.at[0])]
        )
    ]
    for load in loads:
        load.start()
    pl.semaphore_wait(barrier, len(greet))

    hid_copies = [
        remote(x_ref, hid.at[tok], s_hid.at[d], r_hid.at[d], {"tok": other_tok(d)}) for d in toks
    ]
    for copy in hid_copies:
        copy.start()

    slices = [(win_hbm, win), (wout_hbm, wout)]
    own_piece = pl.ds(pl.multiple_of(tok * piece, piece), piece)

    def far_copy(k):
        src, dst = slices[k]
        return remote(
            src.at[own_piece], dst.at[1, own_piece], s_far.at[k], r_w.at[k, 0], far_dev
        )

    def near_copy(k, d):
        dst = slices[k][1]
        return remote(
            dst.at[1, own_piece], dst.at[1, own_piece], s_near.at[k, d], r_w.at[k, d],
            {"tok": other_tok(d)},
        )

    for k in range(2):
        far_copy(k).start()

    def share(k):
        far_copy(k).wait_recv()
        for d in toks:
            near_copy(k, d).start()

    hid[tok] = x_ref[...]
    hidden = x_ref[...].astype(jnp.float32)
    normed = rms_scale(hidden, g1_ref[...]).astype(jnp.bfloat16)
    spot = lax.broadcasted_iota(jnp.int32, (BUCKETS, wide), 1)
    offset = jnp.where(spot < count, spot, spot - wide) - tok * rows
    chosen = lax.broadcasted_iota(jnp.int32, (BUCKETS, wide), 0) == bucket_of(offset)
    bias_line = jnp.dot(
        bias_ref[...], chosen.astype(jnp.float32),
        precision=lax.Precision.HIGHEST, preferred_element_type=jnp.float32,
    )
    loads[0].wait()
    q_scr[...] = jnp.dot(normed, wq[...], preferred_element_type=jnp.float32).astype(jnp.bfloat16)
    loads[1].wait()

    def keys_values(values, who):
        kv_scr[pl.ds(pl.multiple_of(who * rows, rows), rows), :] = jnp.dot(
            values, wkv[...], preferred_element_type=jnp.float32
        ).astype(jnp.bfloat16)

    keys_values(normed, tok)
    for d in toks:
        hid_copies[d - 1].wait_recv()
        who = lax.rem(tok + n_tok - d, n_tok)
        keys_values(
            rms_scale(hid[who].astype(jnp.float32), g1_ref[...]).astype(jnp.bfloat16), who
        )
    own_seg = seg_col_ref[pl.ds(pl.multiple_of(tok * rows, rows), rows), :]
    same = own_seg == seg_row_ref[...]
    low = lax.broadcasted_iota(jnp.int32, (rows, 2 * HD), 1) < HD
    for pair in range(HEADS // 2):
        at = pair * 2 * HD
        q_two = q_scr[:, at:at + 2 * HD]
        k_two = kv_scr[:, at:at + 2 * HD]
        v_two = kv_scr[:, D + at:D + at + 2 * HD]
        halves = []
        for half in range(2):
            head = 2 * pair + half
            keep = low if half == 0 else jnp.logical_not(low)
            q_one = jnp.where(keep, q_two, jnp.zeros_like(q_two))
            scores = lax.dot_general(
                q_one, k_two, (((1,), (1,)), ((), ())), preferred_element_type=jnp.float32
            )
            line = jnp.broadcast_to(bias_line[head:head + 1, :], (rows, wide))
            bias = pltpu.roll(line, 0, 1, stride=1, stride_axis=0)[:, :count]
            masked = jnp.where(same, scores + bias, -1e30)
            top = jnp.max(masked, axis=-1, keepdims=True)
            exps = jnp.exp(masked - top)
            total = jnp.sum(exps, axis=-1, keepdims=True)
            mixed = jnp.dot(exps.astype(jnp.bfloat16), v_two, preferred_element_type=jnp.float32)
            halves.append(mixed / total)
        att_scr[:, at:at + 2 * HD] = jnp.where(low, halves[0], halves[1]).astype(jnp.bfloat16)
    loads[2].wait()
    middle = x_ref[...].astype(jnp.float32) + jnp.dot(
        att_scr[...], wo[...], preferred_element_type=jnp.float32
    )
    mid[...] = middle
    own = place(z, y)
    gath[own, c] = rms_scale(middle, g2_ref[...]).astype(jnp.bfloat16)

    def rows_of(half):
        return pl.ds(half * half_rows, half_rows)

    def pass_on(g, half, ss, to):
        spot = gath.at[g, c, rows_of(half)]
        return remote(spot, spot, ss, r_gath.at[g, c, half], to)

    def z_copy(g, half):
        return pass_on(g, half, s_z.at[g, half], near_dev)

    def y_copy(g, half, d):
        return pass_on(g, half, s_y.at[d, g, half], dev(z, beside(d), c))

    def core_copy(g, half):
        return pass_on(g, half, s_core.at[g, half], core_dev)

    def arrived(g, core, half):
        spot = gath.at[g, core, rows_of(half)]
        remote(spot, spot, s_core.at[g, half], r_gath.at[g, core, half], core_dev).wait_recv()

    near = place(zp, y)
    z_copy(own, 0).start()
    for d in sides:
        y_copy(own, 1, d).start()
    z_copy(own, 1).start()
    for d in sides:
        y_copy(own, 0, d).start()
    for half in range(2):
        core_copy(own, half).start()
    share(0)
    arrived(near, c, 0)
    for d in sides:
        y_copy(near, 0, d).start()
    core_copy(near, 0).start()
    for d in sides:
        g = place(z, beside(d))
        arrived(g, c, 1)
        z_copy(g, 1).start()
        core_copy(g, 1).start()
    share(1)
    arrived(near, c, 1)
    core_copy(near, 1).start()
    for d in sides:
        g = place(z, beside(d))
        arrived(g, c, 0)
        core_copy(g, 0).start()

    def cross_copy(g):
        return remote(part.at[g, oc], cross.at[g], s_cross.at[g], r_cross.at[g], core_dev)

    def multiply(g):
        for half in range(2):
            arrived(g, oc, half)
        tokens = gath[g].reshape(2 * rows, D)
        inner = lax.dot_general(
            tokens, win[...].reshape(-1, D), (((1,), (1,)), ((), ())),
            preferred_element_type=jnp.float32,
        )
        inner = jnp.maximum(inner, 0.0).astype(jnp.bfloat16)
        terms = jnp.dot(inner, wout[...].reshape(-1, D), preferred_element_type=jnp.float32)
        part[g] = terms.astype(jnp.bfloat16).reshape(2, rows, D)
        cross_copy(g).start()

    def both_cores(g, half):
        return part[g, c, rows_of(half)].astype(jnp.float32) + cross[g, rows_of(half)].astype(
            jnp.float32
        )

    def send_sum(kind, d, g, half, to):
        return remote(
            part.at[g, c, rows_of(half)], inbox.at[kind, d], s_out.at[kind, d], r_in.at[kind, d], to
        )

    def corner_a(d):
        return send_sum(0, d, place(zp, beside(d)), 0, dev(z, beside(d), c))

    def corner_b(d):
        return send_sum(1, d, place(zp, beside(d)), 1, near_dev)

    def side_a(d):
        return send_sum(2, d, place(z, beside(d)), 0, dev(z, beside(d), c))

    def near_b():
        return send_sum(3, 0, near, 1, near_dev)

    def near_a():
        return send_sum(4, 0, near, 0, near_dev)

    def side_b(d):
        return send_sum(5, d, place(z, beside(d)), 1, dev(z, beside(d), c))

    def got(kind, d):
        send_sum(kind, d, own, 0, core_dev).wait_recv()
        return inbox[kind, d].astype(jnp.float32)

    def settle(g, half, extra):
        part[g, c, rows_of(half)] = (both_cores(g, half) + extra).astype(jnp.bfloat16)

    loads[3].wait()
    loads[4].wait()
    for k in range(2):
        for d in toks:
            near_copy(k, d).wait_recv()
    multiply(own)
    multiply(near)
    for d in sides:
        multiply(place(z, beside(d)))
    cross_copy(near).wait_recv()
    settle(near, 1, 0.0)
    near_b().start()
    for d in sides:
        g = place(zp, beside(d))
        arrived(g, c, 0)
        core_copy(g, 0).start()
        arrived(g, c, 1)
        core_copy(g, 1).start()
    for d in sides:
        g = place(z, beside(d))
        cross_copy(g).wait_recv()
        settle(g, 0, 0.0)
        side_a(d).start()
    for d in sides:
        multiply(place(zp, beside(d)))
    for d in sides:
        g = place(zp, beside(d))
        cross_copy(g).wait_recv()
        settle(g, 0, 0.0)
        corner_a(d).start()
        settle(g, 1, 0.0)
        corner_b(d).start()
    extra = jnp.zeros((half_rows, D), jnp.float32)
    for d in sides:
        extra = extra + got(0, d)
    settle(near, 0, extra)
    near_a().start()
    for d in sides:
        settle(place(z, beside(d)), 1, got(1, d))
        side_b(d).start()
    cross_copy(own).wait_recv()
    for half in range(2):
        at = rows_of(half)
        total = mid[at, :] + both_cores(own, half)
        for d in sides:
            total = total + got((2, 5)[half], d)
        total = total + got((4, 3)[half], 0)
        out_ref[at, :] = total.astype(jnp.bfloat16)

    for copy in hid_copies:
        copy.wait_send()
    for k in range(2):
        far_copy(k).wait_send()
        for d in toks:
            near_copy(k, d).wait_send()
    for half in range(2):
        z_copy(own, half).wait_send()
        for zz in (z, zp):
            for d in range(WIDE):
                core_copy(place(zz, beside(d)), half).wait_send()
    for d in sides:
        y_copy(own, 0, d).wait_send()
        y_copy(own, 1, d).wait_send()
        y_copy(near, 0, d).wait_send()
        z_copy(place(z, beside(d)), 1).wait_send()
        corner_a(d).wait_send()
        corner_b(d).wait_send()
        side_a(d).wait_send()
        side_b(d).wait_send()
    near_a().wait_send()
    near_b().wait_send()
    for zz in (z, zp):
        for d in range(WIDE):
            cross_copy(place(zz, beside(d))).wait_send()


def per_device(
    n_tok, n_blk, hidden_in, seg_ids, norm_gain1, w_query, w_key_value, rel_bias, w_attn_out,
    norm_gain2, w_in, w_out,
):
    rows = hidden_in.shape[1]
    count = n_tok * rows
    units = w_in.shape[0]
    wide = n_blk // 8
    chips = 2 * wide
    dma = pltpu.SemaphoreType.DMA

    def half(*shape):
        return pltpu.VMEM(shape, jnp.bfloat16)

    out = pl.pallas_call(
        functools.partial(layer_kernel, wide),
        out_shape=jax.ShapeDtypeStruct((rows, D), jnp.bfloat16),
        in_specs=[VM] * 6 + [ANY] * 5,
        out_specs=VM,
        scratch_shapes=[
            half(D, D),
            half(D, 2 * D),
            half(D, D),
            half(2, units, D),
            half(2, units, D),
            half(n_tok, rows, D),
            half(rows, D),
            half(count, 2 * D),
            half(rows, D),
            pltpu.VMEM((rows, D), jnp.float32),
            half(chips, 2, rows, D),
            half(chips, 2, rows, D),
            half(chips, rows, D),
            half(6, wide, rows // 2, D),
            dma((5,)),
            dma((n_tok,)),
            dma((n_tok,)),
            dma((2,)),
            dma((2, n_tok)),
            dma((2, n_tok)),
            dma((chips, 2)),
            dma((wide, chips, 2)),
            dma((chips, 2)),
            dma((chips, 2, 2)),
            dma((chips,)),
            dma((chips,)),
            dma((6, wide)),
            dma((6, wide)),
        ],
        compiler_params=pltpu.CompilerParams(
            collective_id=0, has_side_effects=True, vmem_limit_bytes=60 << 20
        ),
    )(
        hidden_in[0], seg_ids, jnp.transpose(seg_ids), norm_gain1[None], jnp.transpose(rel_bias),
        norm_gain2[None], w_query, w_key_value, w_attn_out, w_in, w_out,
    )
    return out[None]


def solution(mesh):
    placed = (
        P("blk", "tok", None),
        P("blk", None),
        P(),
        P(),
        P(),
        P(),
        P(),
        P(),
        P("blk", None),
        P("blk", None),
    )
    return jax.shard_map(
        functools.partial(per_device, mesh.shape["tok"], mesh.shape["blk"]),
        mesh=mesh, in_specs=placed, out_specs=P("blk", "tok", None), check_vma=False,
    )
```

```python
import functools

import jax
import jax.numpy as jnp
from jax import lax
from jax.experimental import pallas as pl
from jax.experimental.pallas import tpu as pltpu
from jax.sharding import PartitionSpec as P

D = 1024
HEADS = 16
HD = 64
BUCKETS = 32

bucket_bounds = (12, 16, 23, 32, 46, 64, 91)
epsilon = 1e-06
MESH = pl.DeviceIdType.MESH
VM = pl.BlockSpec(memory_space=pltpu.VMEM)
ANY = pl.BlockSpec(memory_space=pl.ANY)


def bucket_of(offset):
    distance = jnp.abs(offset)
    far_bucket = jnp.full_like(distance, 8)
    for boundary in bucket_bounds:
        far_bucket = far_bucket + (distance >= boundary).astype(jnp.int32)
    chosen = jnp.where(distance < 8, distance, far_bucket)
    return chosen + 16 * (offset > 0).astype(jnp.int32)


def rms_scale(values, gain):
    mean_square = jnp.mean(values * values, axis=-1, keepdims=True)
    return values * lax.rsqrt(mean_square + epsilon) * gain


def layer_kernel(
    WIDE,
    x_ref, seg_row_ref, g1_ref, bias_ref, g2_ref, wq_hbm, wkv_hbm, wo_hbm, win_hbm,
    wout_hbm, out_ref,
    wq, wkv, wo, win, wout, hid, q_scr, kv_scr, att_scr, mid, gath, part, cross, inbox, inner_scr,
    s_load, s_hid, r_hid, s_far, s_near, r_w, s_z, s_y, s_core, r_gath, s_cross, r_cross,
    s_out, r_in,
):
    tok = lax.axis_index("tok")
    blk = lax.axis_index("blk")
    c = lax.rem(blk, 2)
    chip = blk // 2
    y = lax.rem(chip, WIDE)
    z = chip // WIDE
    zp = z + 1 - 2 * lax.rem(z, 2)
    zq = lax.rem(z + 2, 4)
    oc = 1 - c
    n_tok, rows, _ = hid.shape
    count = n_tok * rows
    wide = 2 * count
    half_rows = rows // 2
    piece = win_hbm.shape[0] // n_tok

    def dev(zz, yy, cc):
        return {"blk": (zz * WIDE + yy) * 2 + cc}

    def place(zz, yy):
        return lax.rem(zz, 2) * WIDE + yy

    def beside(d):
        return lax.rem(y + d, WIDE)

    def other_tok(d):
        return lax.rem(tok + d, n_tok)

    def remote(src, dst, ss, rs, to):
        return pltpu.make_async_remote_copy(
            src_ref=src, dst_ref=dst, send_sem=ss, recv_sem=rs, device_id=to, device_id_type=MESH
        )

    sides = range(1, WIDE)
    toks = range(1, n_tok)
    core_dev = dev(z, y, oc)
    near_dev = dev(zp, y, c)
    far_dev = dev(zq, y, c)

    barrier = pltpu.get_barrier_semaphore()
    greet = [core_dev, near_dev, far_dev]
    greet += [dev(z, beside(d), c) for d in sides] + [{"tok": other_tok(d)} for d in toks]
    for to in greet:
        pl.semaphore_signal(barrier, inc=1, device_id=to, device_id_type=MESH)

    loads = [
        pltpu.make_async_copy(src, dst, s_load.at[k])
        for k, (src, dst) in enumerate(
            [(wq_hbm, wq), (wkv_hbm, wkv), (wo_hbm, wo), (win_hbm, win.at[0]), (wout_hbm, wout.at[0])]
        )
    ]
    for load in loads:
        load.start()
    pl.semaphore_wait(barrier, len(greet))

    hid_copies = [
        remote(x_ref, hid.at[tok], s_hid.at[d], r_hid.at[d], {"tok": other_tok(d)}) for d in toks
    ]
    for copy in hid_copies:
        copy.start()

    slices = [(win_hbm, win), (wout_hbm, wout)]
    part_rows = piece // 2

    def spot_of(half):
        return pl.ds(pl.multiple_of(tok * piece + half * part_rows, part_rows), part_rows)

    def far_copy(k, half):
        src, dst = slices[k]
        return remote(
            src.at[spot_of(half)], dst.at[1, spot_of(half)], s_far.at[k, half],
            r_w.at[k, half, 0], far_dev,
        )

    def near_copy(k, half, d):
        spot = slices[k][1].at[1, spot_of(half)]
        return remote(
            spot, spot, s_near.at[k, half, d], r_w.at[k, half, d], {"tok": other_tok(d)}
        )

    for half in range(2):
        far_copy(0, half).start()

    def share(k, half):
        far_copy(k, half).wait_recv()
        for d in toks:
            near_copy(k, half, d).start()

    def shared(k):
        for half in range(2):
            for d in toks:
                near_copy(k, half, d).wait_recv()

    hid[tok] = x_ref[...]
    hidden = x_ref[...].astype(jnp.float32)
    normed = rms_scale(hidden, g1_ref[...]).astype(jnp.bfloat16)
    spot = lax.broadcasted_iota(jnp.int32, (BUCKETS, wide), 1)
    offset = jnp.where(spot < count, spot, spot - wide) - tok * rows
    chosen = lax.broadcasted_iota(jnp.int32, (BUCKETS, wide), 0) == bucket_of(offset)
    bias_line = jnp.dot(
        bias_ref[...], chosen.astype(jnp.float32),
        precision=lax.Precision.HIGHEST, preferred_element_type=jnp.float32,
    )
    loads[0].wait()
    q_scr[...] = jnp.dot(normed, wq[...], preferred_element_type=jnp.float32).astype(jnp.bfloat16)
    loads[1].wait()

    def keys_values(values, who):
        kv_scr[pl.ds(pl.multiple_of(who * rows, rows), rows), :] = jnp.dot(
            values, wkv[...], preferred_element_type=jnp.float32
        ).astype(jnp.bfloat16)

    keys_values(normed, tok)
    for d in toks:
        hid_copies[d - 1].wait_recv()
        who = lax.rem(tok + n_tok - d, n_tok)
        keys_values(
            rms_scale(hid[who].astype(jnp.float32), g1_ref[...]).astype(jnp.bfloat16), who
        )
    seg_row = jnp.broadcast_to(seg_row_ref[...].astype(jnp.float32), (rows, count))
    diagonal = lax.broadcasted_iota(jnp.int32, (rows, count), 1) == tok * rows + (
        lax.broadcasted_iota(jnp.int32, (rows, count), 0)
    )
    same = jnp.sum(jnp.where(diagonal, seg_row, 0.0), axis=-1, keepdims=True) == seg_row
    for half in range(2):
        far_copy(1, half).start()
    low = lax.broadcasted_iota(jnp.int32, (rows, 2 * HD), 1) < HD
    for pair in range(HEADS // 2):
        at = pair * 2 * HD
        q_two = q_scr[:, at:at + 2 * HD]
        k_two = kv_scr[:, at:at + 2 * HD]
        v_two = kv_scr[:, D + at:D + at + 2 * HD]
        halves = []
        for half in range(2):
            head = 2 * pair + half
            keep = low if half == 0 else jnp.logical_not(low)
            q_one = jnp.where(keep, q_two, jnp.zeros_like(q_two))
            scores = lax.dot_general(
                q_one, k_two, (((1,), (1,)), ((), ())), preferred_element_type=jnp.float32
            )
            line = jnp.broadcast_to(bias_line[head:head + 1, :], (rows, wide))
            bias = pltpu.roll(line, 0, 1, stride=1, stride_axis=0)[:, :count]
            masked = jnp.where(same, scores + bias, -1e30)
            top = jnp.max(masked, axis=-1, keepdims=True)
            exps = jnp.exp(masked - top)
            total = jnp.sum(exps, axis=-1, keepdims=True)
            mixed = jnp.dot(exps.astype(jnp.bfloat16), v_two, preferred_element_type=jnp.float32)
            halves.append(mixed / total)
        att_scr[:, at:at + 2 * HD] = jnp.where(low, halves[0], halves[1]).astype(jnp.bfloat16)
    loads[2].wait()
    middle = x_ref[...].astype(jnp.float32) + jnp.dot(
        att_scr[...], wo[...], preferred_element_type=jnp.float32
    )
    mid[...] = middle
    own = place(z, y)
    gath[own, c] = rms_scale(middle, g2_ref[...]).astype(jnp.bfloat16)

    def rows_of(half):
        return pl.ds(half * half_rows, half_rows)

    def pass_on(g, half, ss, to):
        spot = gath.at[g, c, rows_of(half)]
        return remote(spot, spot, ss, r_gath.at[g, c, half], to)

    def z_copy(g, half):
        return pass_on(g, half, s_z.at[g, half], near_dev)

    def y_copy(g, half, d):
        return pass_on(g, half, s_y.at[d, g, half], dev(z, beside(d), c))

    def core_copy(g, half):
        return pass_on(g, half, s_core.at[g, half], core_dev)

    def arrived(g, core, half):
        spot = gath.at[g, core, rows_of(half)]
        remote(spot, spot, s_core.at[g, half], r_gath.at[g, core, half], core_dev).wait_recv()

    def first(g, k):
        tokens = gath[g].reshape(2 * rows, D)
        units = win.shape[1]
        inner = lax.dot_general(
            tokens, win[k], (((1,), (1,)), ((), ())), preferred_element_type=jnp.float32
        )
        inner_scr[g, :, k * units:(k + 1) * units] = jnp.maximum(inner, 0.0).astype(jnp.bfloat16)

    def begin(g):
        for half in range(2):
            arrived(g, oc, half)
        first(g, 0)

    def cross_copy(g):
        return remote(part.at[g, oc], cross.at[g], s_cross.at[g], r_cross.at[g], core_dev)

    def second(g):
        terms = jnp.dot(
            inner_scr[g], wout[...].reshape(-1, D), preferred_element_type=jnp.float32
        )
        part[g] = terms.astype(jnp.bfloat16).reshape(2, rows, D)
        cross_copy(g).start()

    def both_cores(g, half):
        return part[g, c, rows_of(half)].astype(jnp.float32) + cross[g, rows_of(half)].astype(
            jnp.float32
        )

    def send_sum(kind, d, g, half, to):
        return remote(
            part.at[g, c, rows_of(half)], inbox.at[kind, d], s_out.at[kind, d], r_in.at[kind, d], to
        )

    def corner_a(d):
        return send_sum(0, d, place(zp, beside(d)), 0, dev(z, beside(d), c))

    def corner_b(d):
        return send_sum(1, d, place(zp, beside(d)), 1, near_dev)

    def side_a(d):
        return send_sum(2, d, place(z, beside(d)), 0, dev(z, beside(d), c))

    def near_b():
        return send_sum(3, 0, near, 1, near_dev)

    def near_a():
        return send_sum(4, 0, near, 0, near_dev)

    def side_b(d):
        return send_sum(5, d, place(z, beside(d)), 1, dev(z, beside(d), c))

    def got(kind, d):
        send_sum(kind, d, own, 0, core_dev).wait_recv()
        return inbox[kind, d].astype(jnp.float32)

    def settle(g, half, extra):
        part[g, c, rows_of(half)] = (both_cores(g, half) + extra).astype(jnp.bfloat16)

    near = place(zp, y)
    side_chips = [place(z, beside(d)) for d in sides]
    corners = [place(zp, beside(d)) for d in sides]
    z_copy(own, 0).start()
    for d in sides:
        y_copy(own, 1, d).start()
    z_copy(own, 1).start()
    for d in sides:
        y_copy(own, 0, d).start()
    for half in range(2):
        core_copy(own, half).start()
    loads[3].wait()
    begin(own)
    share(0, 0)
    arrived(near, c, 0)
    for d in sides:
        y_copy(near, 0, d).start()
    core_copy(near, 0).start()
    for g in side_chips:
        arrived(g, c, 1)
        z_copy(g, 1).start()
        core_copy(g, 1).start()
    share(0, 1)
    arrived(near, c, 1)
    core_copy(near, 1).start()
    for g in side_chips:
        arrived(g, c, 0)
        core_copy(g, 0).start()
    share(1, 0)
    begin(near)
    for g in side_chips:
        begin(g)
    share(1, 1)
    for g in corners:
        for half in range(2):
            arrived(g, c, half)
            core_copy(g, half).start()
    shared(0)
    first(near, 1)
    for g in side_chips:
        first(g, 1)
    for g in corners:
        begin(g)
        first(g, 1)
    loads[4].wait()
    shared(1)
    for g in corners:
        second(g)
    second(near)
    for d in sides:
        g = corners[d - 1]
        cross_copy(g).wait_recv()
        settle(g, 0, 0.0)
        corner_a(d).start()
        settle(g, 1, 0.0)
        corner_b(d).start()
    for g in side_chips:
        second(g)
    cross_copy(near).wait_recv()
    settle(near, 1, 0.0)
    near_b().start()
    for d in sides:
        g = side_chips[d - 1]
        cross_copy(g).wait_recv()
        settle(g, 0, 0.0)
        side_a(d).start()
    first(own, 1)
    second(own)
    extra = jnp.zeros((half_rows, D), jnp.float32)
    for d in sides:
        extra = extra + got(0, d)
    settle(near, 0, extra)
    near_a().start()
    for d in sides:
        settle(place(z, beside(d)), 1, got(1, d))
        side_b(d).start()
    cross_copy(own).wait_recv()
    for half in range(2):
        at = rows_of(half)
        total = mid[at, :] + both_cores(own, half)
        for d in sides:
            total = total + got((2, 5)[half], d)
        total = total + got((4, 3)[half], 0)
        out_ref[at, :] = total.astype(jnp.bfloat16)

    for copy in hid_copies:
        copy.wait_send()
    for k in range(2):
        for half in range(2):
            far_copy(k, half).wait_send()
            for d in toks:
                near_copy(k, half, d).wait_send()
    for half in range(2):
        z_copy(own, half).wait_send()
        for zz in (z, zp):
            for d in range(WIDE):
                core_copy(place(zz, beside(d)), half).wait_send()
    for d in sides:
        y_copy(own, 0, d).wait_send()
        y_copy(own, 1, d).wait_send()
        y_copy(near, 0, d).wait_send()
        z_copy(place(z, beside(d)), 1).wait_send()
        corner_a(d).wait_send()
        corner_b(d).wait_send()
        side_a(d).wait_send()
        side_b(d).wait_send()
    near_a().wait_send()
    near_b().wait_send()
    for zz in (z, zp):
        for d in range(WIDE):
            cross_copy(place(zz, beside(d))).wait_send()


def per_device(
    n_tok, n_blk, hidden_in, seg_ids, norm_gain1, w_query, w_key_value, rel_bias, w_attn_out,
    norm_gain2, w_in, w_out,
):
    rows = hidden_in.shape[1]
    count = n_tok * rows
    units = w_in.shape[0]
    wide = n_blk // 8
    chips = 2 * wide
    dma = pltpu.SemaphoreType.DMA

    def half(*shape):
        return pltpu.VMEM(shape, jnp.bfloat16)

    out = pl.pallas_call(
        functools.partial(layer_kernel, wide),
        out_shape=jax.ShapeDtypeStruct((rows, D), jnp.bfloat16),
        in_specs=[VM] * 5 + [ANY] * 5,
        out_specs=VM,
        scratch_shapes=[
            half(D, D),
            half(D, 2 * D),
            half(D, D),
            half(2, units, D),
            half(2, units, D),
            half(n_tok, rows, D),
            half(rows, D),
            half(count, 2 * D),
            half(rows, D),
            pltpu.VMEM((rows, D), jnp.float32),
            half(chips, 2, rows, D),
            half(chips, 2, rows, D),
            half(chips, rows, D),
            half(6, wide, rows // 2, D),
            half(chips, 2 * rows, 2 * units),
            dma((5,)),
            dma((n_tok,)),
            dma((n_tok,)),
            dma((2, 2)),
            dma((2, 2, n_tok)),
            dma((2, 2, n_tok)),
            dma((chips, 2)),
            dma((wide, chips, 2)),
            dma((chips, 2)),
            dma((chips, 2, 2)),
            dma((chips,)),
            dma((chips,)),
            dma((6, wide)),
            dma((6, wide)),
        ],
        compiler_params=pltpu.CompilerParams(
            collective_id=0, has_side_effects=True, vmem_limit_bytes=60 << 20
        ),
    )(
        hidden_in[0], seg_ids, norm_gain1[None], jnp.transpose(rel_bias),
        norm_gain2[None], w_query, w_key_value, w_attn_out, w_in, w_out,
    )
    return out[None]


def solution(mesh):
    placed = (
        P("blk", "tok", None),
        P("blk", None),
        P(),
        P(),
        P(),
        P(),
        P(),
        P(),
        P("blk", None),
        P("blk", None),
    )
    return jax.shard_map(
        functools.partial(per_device, mesh.shape["tok"], mesh.shape["blk"]),
        mesh=mesh, in_specs=placed, out_specs=P("blk", "tok", None), check_vma=False,
    )
```

```python
import functools

import jax
import jax.numpy as jnp
from jax import lax
from jax.experimental import pallas as pl
from jax.experimental.pallas import tpu as pltpu
from jax.sharding import PartitionSpec as P

D = 1024
HEADS = 16
HD = 64
BUCKETS = 32

bucket_bounds = (12, 16, 23, 32, 46, 64, 91)
epsilon = 1e-06
MESH = pl.DeviceIdType.MESH
VM = pl.BlockSpec(memory_space=pltpu.VMEM)
ANY = pl.BlockSpec(memory_space=pl.ANY)


def bucket_of(offset):
    distance = jnp.abs(offset)
    far_bucket = jnp.full_like(distance, 8)
    for boundary in bucket_bounds:
        far_bucket = far_bucket + (distance >= boundary).astype(jnp.int32)
    chosen = jnp.where(distance < 8, distance, far_bucket)
    return chosen + 16 * (offset > 0).astype(jnp.int32)


def rms_scale(values, gain):
    mean_square = jnp.mean(values * values, axis=-1, keepdims=True)
    return values * lax.rsqrt(mean_square + epsilon) * gain


def layer_kernel(
    WIDE,
    x_ref, seg_row_ref, g1_ref, bias_ref, g2_ref, wq_hbm, wkv_hbm, wo_hbm, win_hbm,
    wout_hbm, out_ref,
    wq, wkv, wo, win, wout, hid, q_scr, kv_scr, att_scr, mid, gath, part, cross, inbox, inner_scr,
    s_load, s_hid, r_hid, s_far, s_near, r_w, s_z, s_y, s_core, r_gath, s_cross, r_cross,
    s_out, r_in,
):
    tok = lax.axis_index("tok")
    blk = lax.axis_index("blk")
    c = lax.rem(blk, 2)
    chip = blk // 2
    y = lax.rem(chip, WIDE)
    z = chip // WIDE
    zp = z + 1 - 2 * lax.rem(z, 2)
    zq = lax.rem(z + 2, 4)
    oc = 1 - c
    n_tok, rows, _ = hid.shape
    count = n_tok * rows
    wide = 2 * count
    half_rows = rows // 2
    piece = win_hbm.shape[0] // n_tok

    def dev(zz, yy, cc):
        return {"blk": (zz * WIDE + yy) * 2 + cc}

    def place(zz, yy):
        return lax.rem(zz, 2) * WIDE + yy

    def beside(d):
        return lax.rem(y + d, WIDE)

    def other_tok(d):
        return lax.rem(tok + d, n_tok)

    def remote(src, dst, ss, rs, to):
        return pltpu.make_async_remote_copy(
            src_ref=src, dst_ref=dst, send_sem=ss, recv_sem=rs, device_id=to, device_id_type=MESH
        )

    sides = range(1, WIDE)
    toks = range(1, n_tok)
    core_dev = dev(z, y, oc)
    near_dev = dev(zp, y, c)
    far_dev = dev(zq, y, c)

    barrier = pltpu.get_barrier_semaphore()
    greet = [core_dev, near_dev, far_dev]
    greet += [dev(z, beside(d), c) for d in sides] + [{"tok": other_tok(d)} for d in toks]
    for to in greet:
        pl.semaphore_signal(barrier, inc=1, device_id=to, device_id_type=MESH)

    loads = [
        pltpu.make_async_copy(src, dst, s_load.at[k])
        for k, (src, dst) in enumerate(
            [(wq_hbm, wq), (wkv_hbm, wkv), (wo_hbm, wo), (win_hbm, win.at[0]), (wout_hbm, wout.at[0])]
        )
    ]
    for load in loads:
        load.start()
    pl.semaphore_wait(barrier, len(greet))

    hid_copies = [
        remote(x_ref, hid.at[tok], s_hid.at[d], r_hid.at[d], {"tok": other_tok(d)}) for d in toks
    ]
    for copy in hid_copies:
        copy.start()

    slices = [(win_hbm, win), (wout_hbm, wout)]
    part_rows = piece // 2

    def spot_of(half):
        return pl.ds(pl.multiple_of(tok * piece + half * part_rows, part_rows), part_rows)

    def far_copy(k, half):
        src, dst = slices[k]
        return remote(
            src.at[spot_of(half)], dst.at[1, spot_of(half)], s_far.at[k, half],
            r_w.at[k, half, 0], far_dev,
        )

    def near_copy(k, half, d):
        spot = slices[k][1].at[1, spot_of(half)]
        return remote(
            spot, spot, s_near.at[k, half, d], r_w.at[k, half, d], {"tok": other_tok(d)}
        )

    for k in range(2):
        for half in range(2):
            far_copy(k, half).start()

    def share(k, half):
        far_copy(k, half).wait_recv()
        for d in toks:
            near_copy(k, half, d).start()

    def shared(k):
        for half in range(2):
            for d in toks:
                near_copy(k, half, d).wait_recv()

    hid[tok] = x_ref[...]
    hidden = x_ref[...].astype(jnp.float32)
    normed = rms_scale(hidden, g1_ref[...]).astype(jnp.bfloat16)
    spot = lax.broadcasted_iota(jnp.int32, (BUCKETS, wide), 1)
    offset = jnp.where(spot < count, spot, spot - wide) - tok * rows
    chosen = lax.broadcasted_iota(jnp.int32, (BUCKETS, wide), 0) == bucket_of(offset)
    bias_line = jnp.dot(
        bias_ref[...], chosen.astype(jnp.float32),
        precision=lax.Precision.HIGHEST, preferred_element_type=jnp.float32,
    )
    loads[0].wait()
    q_scr[...] = jnp.dot(normed, wq[...], preferred_element_type=jnp.float32).astype(jnp.bfloat16)
    loads[1].wait()

    def keys_values(values, who):
        kv_scr[pl.ds(pl.multiple_of(who * rows, rows), rows), :] = jnp.dot(
            values, wkv[...], preferred_element_type=jnp.float32
        ).astype(jnp.bfloat16)

    keys_values(normed, tok)
    for d in toks:
        hid_copies[d - 1].wait_recv()
        who = lax.rem(tok + n_tok - d, n_tok)
        keys_values(
            rms_scale(hid[who].astype(jnp.float32), g1_ref[...]).astype(jnp.bfloat16), who
        )
    seg_row = jnp.broadcast_to(seg_row_ref[...].astype(jnp.float32), (rows, count))
    diagonal = lax.broadcasted_iota(jnp.int32, (rows, count), 1) == tok * rows + (
        lax.broadcasted_iota(jnp.int32, (rows, count), 0)
    )
    same = jnp.sum(jnp.where(diagonal, seg_row, 0.0), axis=-1, keepdims=True) == seg_row
    low = lax.broadcasted_iota(jnp.int32, (rows, 2 * HD), 1) < HD
    for pair in range(HEADS // 2):
        at = pair * 2 * HD
        q_two = q_scr[:, at:at + 2 * HD]
        k_two = kv_scr[:, at:at + 2 * HD]
        v_two = kv_scr[:, D + at:D + at + 2 * HD]
        halves = []
        for half in range(2):
            head = 2 * pair + half
            keep = low if half == 0 else jnp.logical_not(low)
            q_one = jnp.where(keep, q_two, jnp.zeros_like(q_two))
            scores = lax.dot_general(
                q_one, k_two, (((1,), (1,)), ((), ())), preferred_element_type=jnp.float32
            )
            line = jnp.broadcast_to(bias_line[head:head + 1, :], (rows, wide))
            bias = pltpu.roll(line, 0, 1, stride=1, stride_axis=0)[:, :count]
            masked = jnp.where(same, scores + bias, -1e30)
            top = jnp.max(masked, axis=-1, keepdims=True)
            exps = jnp.exp(masked - top)
            total = jnp.sum(exps, axis=-1, keepdims=True)
            mixed = jnp.dot(exps.astype(jnp.bfloat16), v_two, preferred_element_type=jnp.float32)
            halves.append(mixed / total)
        att_scr[:, at:at + 2 * HD] = jnp.where(low, halves[0], halves[1]).astype(jnp.bfloat16)
    loads[2].wait()
    middle = x_ref[...].astype(jnp.float32) + jnp.dot(
        att_scr[...], wo[...], preferred_element_type=jnp.float32
    )
    mid[...] = middle
    own = place(z, y)
    gath[own, c] = rms_scale(middle, g2_ref[...]).astype(jnp.bfloat16)

    def rows_of(half):
        return pl.ds(half * half_rows, half_rows)

    def pass_on(g, half, ss, to):
        spot = gath.at[g, c, rows_of(half)]
        return remote(spot, spot, ss, r_gath.at[g, c, half], to)

    def z_copy(g, half):
        return pass_on(g, half, s_z.at[g, half], near_dev)

    def y_copy(g, half, d):
        return pass_on(g, half, s_y.at[d, g, half], dev(z, beside(d), c))

    def core_copy(g, half):
        return pass_on(g, half, s_core.at[g, half], core_dev)

    def arrived(g, core, half):
        spot = gath.at[g, core, rows_of(half)]
        remote(spot, spot, s_core.at[g, half], r_gath.at[g, core, half], core_dev).wait_recv()

    def first(g, k):
        tokens = gath[g].reshape(2 * rows, D)
        units = win.shape[1]
        inner = lax.dot_general(
            tokens, win[k], (((1,), (1,)), ((), ())), preferred_element_type=jnp.float32
        )
        inner_scr[g, :, k * units:(k + 1) * units] = jnp.maximum(inner, 0.0).astype(jnp.bfloat16)

    def begin(g):
        for half in range(2):
            arrived(g, oc, half)
        first(g, 0)

    def cross_copy(g):
        return remote(part.at[g, oc], cross.at[g], s_cross.at[g], r_cross.at[g], core_dev)

    def second(g):
        terms = jnp.dot(
            inner_scr[g], wout[...].reshape(-1, D), preferred_element_type=jnp.float32
        )
        part[g] = terms.astype(jnp.bfloat16).reshape(2, rows, D)
        cross_copy(g).start()

    def both_cores(g, half):
        return part[g, c, rows_of(half)].astype(jnp.float32) + cross[g, rows_of(half)].astype(
            jnp.float32
        )

    def send_sum(kind, d, g, half, to):
        return remote(
            part.at[g, c, rows_of(half)], inbox.at[kind, d], s_out.at[kind, d], r_in.at[kind, d], to
        )

    def corner_a(d):
        return send_sum(0, d, place(zp, beside(d)), 0, dev(z, beside(d), c))

    def corner_b(d):
        return send_sum(1, d, place(zp, beside(d)), 1, near_dev)

    def side_a(d):
        return send_sum(2, d, place(z, beside(d)), 0, dev(z, beside(d), c))

    def near_b():
        return send_sum(3, 0, near, 1, near_dev)

    def near_a():
        return send_sum(4, 0, near, 0, near_dev)

    def side_b(d):
        return send_sum(5, d, place(z, beside(d)), 1, dev(z, beside(d), c))

    def got(kind, d):
        send_sum(kind, d, own, 0, core_dev).wait_recv()
        return inbox[kind, d].astype(jnp.float32)

    def settle(g, half, extra):
        part[g, c, rows_of(half)] = (both_cores(g, half) + extra).astype(jnp.bfloat16)

    near = place(zp, y)
    side_chips = [place(z, beside(d)) for d in sides]
    corners = [place(zp, beside(d)) for d in sides]
    z_copy(own, 0).start()
    for d in sides:
        y_copy(own, 1, d).start()
    z_copy(own, 1).start()
    for d in sides:
        y_copy(own, 0, d).start()
    for half in range(2):
        core_copy(own, half).start()
    loads[3].wait()
    begin(own)
    share(0, 0)
    arrived(near, c, 0)
    for d in sides:
        y_copy(near, 0, d).start()
    core_copy(near, 0).start()
    for g in side_chips:
        arrived(g, c, 1)
        z_copy(g, 1).start()
        core_copy(g, 1).start()
    share(0, 1)
    arrived(near, c, 1)
    core_copy(near, 1).start()
    for g in side_chips:
        arrived(g, c, 0)
        core_copy(g, 0).start()
    share(1, 0)
    begin(near)
    for g in side_chips:
        begin(g)
    share(1, 1)
    for g in corners:
        for half in range(2):
            arrived(g, c, half)
            core_copy(g, half).start()
    shared(0)
    first(near, 1)
    for g in side_chips:
        first(g, 1)
    for g in corners:
        begin(g)
        first(g, 1)
    loads[4].wait()
    shared(1)
    for g in corners:
        second(g)
    second(near)
    for d in sides:
        g = corners[d - 1]
        cross_copy(g).wait_recv()
        settle(g, 0, 0.0)
        corner_a(d).start()
        settle(g, 1, 0.0)
        corner_b(d).start()
    for g in side_chips:
        second(g)
    cross_copy(near).wait_recv()
    settle(near, 1, 0.0)
    near_b().start()
    for d in sides:
        g = side_chips[d - 1]
        cross_copy(g).wait_recv()
        settle(g, 0, 0.0)
        side_a(d).start()
    first(own, 1)
    second(own)
    extra = jnp.zeros((half_rows, D), jnp.float32)
    for d in sides:
        extra = extra + got(0, d)
    settle(near, 0, extra)
    near_a().start()
    for d in sides:
        settle(place(z, beside(d)), 1, got(1, d))
        side_b(d).start()
    cross_copy(own).wait_recv()
    for half in range(2):
        at = rows_of(half)
        total = mid[at, :] + both_cores(own, half)
        for d in sides:
            total = total + got((2, 5)[half], d)
        total = total + got((4, 3)[half], 0)
        out_ref[at, :] = total.astype(jnp.bfloat16)

    for copy in hid_copies:
        copy.wait_send()
    for k in range(2):
        for half in range(2):
            far_copy(k, half).wait_send()
            for d in toks:
                near_copy(k, half, d).wait_send()
    for half in range(2):
        z_copy(own, half).wait_send()
        for zz in (z, zp):
            for d in range(WIDE):
                core_copy(place(zz, beside(d)), half).wait_send()
    for d in sides:
        y_copy(own, 0, d).wait_send()
        y_copy(own, 1, d).wait_send()
        y_copy(near, 0, d).wait_send()
        z_copy(place(z, beside(d)), 1).wait_send()
        corner_a(d).wait_send()
        corner_b(d).wait_send()
        side_a(d).wait_send()
        side_b(d).wait_send()
    near_a().wait_send()
    near_b().wait_send()
    for zz in (z, zp):
        for d in range(WIDE):
            cross_copy(place(zz, beside(d))).wait_send()


def per_device(
    n_tok, n_blk, hidden_in, seg_ids, norm_gain1, w_query, w_key_value, rel_bias, w_attn_out,
    norm_gain2, w_in, w_out,
):
    rows = hidden_in.shape[1]
    count = n_tok * rows
    units = w_in.shape[0]
    wide = n_blk // 8
    chips = 2 * wide
    dma = pltpu.SemaphoreType.DMA

    def half(*shape):
        return pltpu.VMEM(shape, jnp.bfloat16)

    out = pl.pallas_call(
        functools.partial(layer_kernel, wide),
        out_shape=jax.ShapeDtypeStruct((rows, D), jnp.bfloat16),
        in_specs=[VM] * 5 + [ANY] * 5,
        out_specs=VM,
        scratch_shapes=[
            half(D, D),
            half(D, 2 * D),
            half(D, D),
            half(2, units, D),
            half(2, units, D),
            half(n_tok, rows, D),
            half(rows, D),
            half(count, 2 * D),
            half(rows, D),
            pltpu.VMEM((rows, D), jnp.float32),
            half(chips, 2, rows, D),
            half(chips, 2, rows, D),
            half(chips, rows, D),
            half(6, wide, rows // 2, D),
            half(chips, 2 * rows, 2 * units),
            dma((5,)),
            dma((n_tok,)),
            dma((n_tok,)),
            dma((2, 2)),
            dma((2, 2, n_tok)),
            dma((2, 2, n_tok)),
            dma((chips, 2)),
            dma((wide, chips, 2)),
            dma((chips, 2)),
            dma((chips, 2, 2)),
            dma((chips,)),
            dma((chips,)),
            dma((6, wide)),
            dma((6, wide)),
        ],
        compiler_params=pltpu.CompilerParams(
            collective_id=0, has_side_effects=True, vmem_limit_bytes=60 << 20
        ),
    )(
        hidden_in[0], seg_ids, norm_gain1[None], jnp.transpose(rel_bias),
        norm_gain2[None], w_query, w_key_value, w_attn_out, w_in, w_out,
    )
    return out[None]


def solution(mesh):
    placed = (
        P("blk", "tok", None),
        P("blk", None),
        P(),
        P(),
        P(),
        P(),
        P(),
        P(),
        P("blk", None),
        P("blk", None),
    )
    return jax.shard_map(
        functools.partial(per_device, mesh.shape["tok"], mesh.shape["blk"]),
        mesh=mesh, in_specs=placed, out_specs=P("blk", "tok", None), check_vma=False,
    )
```
